128 devices in a mesh: kv: 8 (over x, z_hi), seq: 16 (over y, z_lo, core).
Axes of the slice: x: 4, y: 4, z: 4 (z_hi: 2, z_lo: 2; z = z_hi * 2 + z_lo), core: 2. Of those that a mesh axis runs over, the one named last changes fastest.
Arguments:
- queries: bfloat16 [4096, 16384], P('seq', 'kv'), may hold values from -24 to 24
- keys: bfloat16 [4096, 1024], P('seq', 'kv'), may hold values from -24 to 24
- values: bfloat16 [4096, 1024], P('seq', 'kv'), may hold values from -6 to 6
- query_map: float32 [128, 128, 64], P('kv'), may hold values from -4 to 4
- key_map: float32 [128, 128, 64], P('kv'), may hold values from -4 to 4
Outputs:
- grad_query_map: float32 [128, 128, 64], P(('kv', 'seq'))
- grad_key_map: float32 [128, 128, 64], P(('kv', 'seq'))
The draws below stay inside these ranges and needn't reach their ends.
All inputs are finite; a program needn't handle non-finite values.
Results may differ from the reference program's by a relative error of at most 0.00165.
Values may be sent and summed in bfloat16 or wider, within the bound.
No kernel may reach another device: no remote copies, remote signals or barrier semaphores. Data moves between devices by JAX's collectives and lax.ppermute only.
A program may use at most 128 MiB of HBM per device.

```python
import jax
import jax.numpy as jnp
from jax import lax

HQ = 128
KVH = 8
HD = 128
FMAP = 64
LENGTH = 4096
GROUP = 16


def teacher_pair(key):
    queries = jax.random.normal(jax.random.fold_in(key, 11), (LENGTH, HQ * HD), jnp.float32)
    keys = jax.random.normal(jax.random.fold_in(key, 12), (LENGTH, KVH * HD), jnp.float32)
    return (jnp.clip(queries, -24.0, 24.0), jnp.clip(keys, -24.0, 24.0))


def draw_queries(key, part):
    return teacher_pair(key)[0].astype(jnp.bfloat16)


def draw_keys(key, part):
    return teacher_pair(key)[1].astype(jnp.bfloat16)


def map_weights(key, salt):
    weights = jax.random.normal(jax.random.fold_in(key, salt), (HQ, HD, FMAP), jnp.float32) * HD ** (-0.5)
    return jnp.clip(weights, -4.0, 4.0)


def draw_query_map(key, part):
    return map_weights(key, 21)


def draw_key_map(key, part):
    return map_weights(key, 22)


def level_of(key, extent, cuts, smallest, top_value):
    def one(dim, blocks):
        draws = jax.random.uniform(jax.random.fold_in(jax.random.fold_in(key, 6), dim), (blocks,), jnp.float32, smallest / len(cuts), top_value / len(cuts))
        return jnp.repeat(jnp.exp(draws), extent[dim] // blocks).reshape((-1,) + (1,) * (len(extent) - dim - 1))

    level = one(*cuts[0])
    for cut in cuts[1:]:
        level = level * one(*cut)
    return level


def noise(rng, dims, scale, reach, pieces=(), kind=jnp.bfloat16):
    drawn = jax.random.normal(rng, dims, jnp.float32) * scale
    if len(pieces) > 0:
        drawn = level_of(rng, dims, pieces, -0.22, 0.18) * drawn
    return jnp.clip(drawn, min=-reach, max=reach).astype(kind)


def setup_inputs(seed: int = 0) -> dict:
    arg_keys = jax.random.split(jax.random.key(seed), 6)
    queries = draw_queries(jax.random.fold_in(arg_keys[5], 71), 0)
    keys = draw_keys(jax.random.fold_in(arg_keys[5], 71), 0)
    values = noise(arg_keys[2], (LENGTH, KVH * HD), 1.0, 6.0, ((0, 16), (1, 8)))
    query_map = draw_query_map(jax.random.fold_in(arg_keys[5], 71), 0)
    key_map = draw_key_map(jax.random.fold_in(arg_keys[5], 71), 0)
    return {"queries": queries, "keys": keys, "values": values, "query_map": query_map, "key_map": key_map}


def block_size(count):
    return max((d for d in range(1, min(count, 512) + 1) if count % d == 0))

def feature(logits):
    return jnp.concatenate([jax.nn.softmax(logits, axis=-1), jax.nn.softmax(-logits, axis=-1)], axis=-1)

def reference(queries, keys, values, query_map, key_map):
    qblock = block_size(LENGTH)
    nblocks = LENGTH // qblock
    scale = 1.0 / HD ** 0.5
    hi = lax.Precision.HIGHEST
    positions = jnp.arange(LENGTH, dtype=jnp.int32)

    def per_group(group_id):
        qg = lax.dynamic_slice_in_dim(queries, group_id * GROUP * HD, GROUP * HD, 1).reshape(LENGTH, GROUP, HD)
        kg = lax.dynamic_slice_in_dim(keys, group_id * HD, HD, 1)
        vg = lax.dynamic_slice_in_dim(values, group_id * HD, HD, 1)
        wq = lax.dynamic_slice_in_dim(query_map, group_id * GROUP, GROUP, 0)
        wk = lax.dynamic_slice_in_dim(key_map, group_id * GROUP, GROUP, 0)
        kf = kg.astype(jnp.float32)
        vf = vg.astype(jnp.float32)

        def teacher_block(index):
            qb = lax.dynamic_slice_in_dim(qg, index * qblock, qblock, 0).astype(jnp.float32)
            scores = jnp.einsum('tjd,sd->jts', qb, kf, precision=hi) * scale
            qpos = index * qblock + jnp.arange(qblock, dtype=jnp.int32)
            allowed = positions[None, :] <= qpos[:, None]
            peak = lax.optimization_barrier(jnp.max(jnp.where(allowed[None], scores, -1e+30), axis=-1))
            probs = jnp.where(allowed[None], jnp.exp(scores - peak[..., None]), 0.0)
            total = lax.optimization_barrier(jnp.sum(probs, axis=-1))
            mixed = jnp.einsum('jts,sd->tjd', probs, vf, precision=hi)
            return (mixed / total.T[..., None]).astype(jnp.bfloat16)
        teacher = lax.map(teacher_block, jnp.arange(nblocks, dtype=jnp.int32)).reshape(LENGTH, GROUP, HD)
        target = teacher.astype(jnp.float32)

        def loss_of(wq_in, wk_in):
            fq = feature(jnp.einsum('tjd,jdf->tjf', qg.astype(jnp.float32), wq_in, precision=hi))
            fk = feature(jnp.einsum('sd,jdf->sjf', kf, wk_in, precision=hi))
            lower = (jnp.arange(qblock)[:, None] >= jnp.arange(qblock)[None, :]).astype(jnp.float32)

            def step(carry, index):
                state, norm_sum, loss = carry
                fqb = lax.dynamic_slice_in_dim(fq, index * qblock, qblock, 0)
                fkb = lax.dynamic_slice_in_dim(fk, index * qblock, qblock, 0)
                vb = lax.dynamic_slice_in_dim(vf, index * qblock, qblock, 0)
                ob = lax.dynamic_slice_in_dim(target, index * qblock, qblock, 0)
                attn = jnp.einsum('tjf,sjf->jts', fqb, fkb, precision=hi) * lower[None]
                numer = jnp.einsum('jts,sd->tjd', attn, vb, precision=hi) + jnp.einsum('tjf,jfd->tjd', fqb, state, precision=hi)
                denom = lax.optimization_barrier(jnp.sum(attn, axis=-1)).T + jnp.einsum('tjf,jf->tj', fqb, norm_sum, precision=hi)
                student = numer / denom[..., None]
                loss = loss + jnp.sum((student - ob) ** 2)
                state = state + jnp.einsum('sjf,sd->jfd', fkb, vb, precision=hi)
                norm_sum = norm_sum + lax.optimization_barrier(jnp.sum(fkb, axis=0))
                return ((state, norm_sum, loss), None)
            start = (jnp.zeros((GROUP, 2 * FMAP, HD), jnp.float32), jnp.zeros((GROUP, 2 * FMAP), jnp.float32), jnp.zeros((), jnp.float32))
            final, _ = lax.scan(step, start, jnp.arange(nblocks, dtype=jnp.int32))
            return final[2] / LENGTH
        _, pullback = jax.vjp(loss_of, wq, wk)
        grad_q, grad_k = pullback(jnp.ones((), jnp.float32))
        return (grad_q, grad_k)
    grads_q, grads_k = lax.map(per_group, jnp.arange(KVH, dtype=jnp.int32))
    return (grads_q.reshape(HQ, HD, FMAP), grads_k.reshape(HQ, HD, FMAP))
```

```python
import functools

import jax
import jax.numpy as jnp
from jax import lax
from jax.experimental import pallas as pl
from jax.experimental.pallas import tpu as pltpu
from jax.sharding import PartitionSpec as P

f32, bf16 = jnp.float32, jnp.bfloat16
HD = 128
FEAT = 64
CHUNK = 256
TOGETHER = 8
NT = (((1,), (1,)), ((), ()))
NN = (((1,), (0,)), ((), ()))
TN = (((0,), (0,)), ((), ()))


def dot(a, b, dims=NN):
    return lax.dot_general(a, b, dims, preferred_element_type=f32)


def lanes(*xs):
    return jnp.concatenate(xs, axis=1)


def rows(*xs):
    return jnp.concatenate(xs, axis=0)


def split(x):
    high = x.astype(bf16)
    return high, (x - high.astype(f32)).astype(bf16)


def first_half(shape):
    return lax.broadcasted_iota(jnp.int32, shape, 1) < FEAT


def half_sums(x):
    lo = first_half(x.shape)
    a = jnp.sum(jnp.where(lo, x, 0.0), axis=1, keepdims=True)
    b = jnp.sum(jnp.where(lo, 0.0, x), axis=1, keepdims=True)
    return a, b


def phi(logits):
    lo = first_half(logits.shape)
    a = jnp.max(jnp.where(lo, logits, -jnp.inf), axis=1, keepdims=True)
    b = jnp.max(jnp.where(lo, -jnp.inf, logits), axis=1, keepdims=True)
    e = jnp.exp(logits - jnp.where(lo, a, b))
    a, b = half_sums(e)
    return e * jnp.where(lo, 1.0 / a, 1.0 / b)


def phi_back(p, d):
    x = p * d
    a, b = half_sums(x)
    return x - p * jnp.where(first_half(x.shape), a, b)


def signed_pair(w):
    return rows(*split(lanes(w, -w)))


def lane_max(s):
    m = s[:, :128]
    for at in range(128, s.shape[1], 128):
        m = jnp.maximum(m, s[:, at : at + 128])
    return m


def teacher_kernel(x_ref, o_ref, score, *, block):
    total = x_ref.shape[0]
    exponent = 1.4426950408889634 / HD**0.5

    def scores(i):
        q = x_ref[i * block : (i + 1) * block, :HD]
        peak = None
        for j in range(i + 1):
            s = dot(q, x_ref[j * block : (j + 1) * block, HD : 2 * HD], NT)
            if j == i:
                r = lax.broadcasted_iota(jnp.int32, s.shape, 0)
                c = lax.broadcasted_iota(jnp.int32, s.shape, 1)
                s = jnp.where(r >= c, s, -1e30)
            score[i % 2, :, j * block : (j + 1) * block] = s
            m = lane_max(s)
            peak = m if peak is None else jnp.maximum(peak, m)
        return jnp.max(peak, axis=1, keepdims=True)

    def mix(i, peak):
        n = (i + 1) * block
        ve = lanes(x_ref[:n, 2 * HD :], jnp.ones((n, 128), bf16))
        shift = peak * exponent
        p = [
            jnp.exp2(score[i % 2, :, j * block : (j + 1) * block] * exponent - shift)
            for j in range(i + 1)
        ]
        if i == 0:
            high, low = split(p[0])
            acc = dot(lanes(high, low), rows(ve, ve))
        else:
            acc = dot(lanes(*(x.astype(bf16) for x in p)), ve)
        o_ref[i * block : (i + 1) * block, :] = (acc[:, :HD] / acc[:, HD:]).astype(bf16)

    peak = scores(0)
    for i in range(total // block):
        following = scores(i + 1) if (i + 1) * block < total else None
        mix(i, peak)
        peak = following


def teacher(x):
    total = x.shape[0]
    return pl.pallas_call(
        functools.partial(teacher_kernel, block=CHUNK),
        out_shape=jax.ShapeDtypeStruct((total, HD), bf16),
        scratch_shapes=[pltpu.VMEM((2, CHUNK, total), f32)],
        compiler_params=pltpu.CompilerParams(vmem_limit_bytes=56 << 20),
        name="teacher",
    )(x)


def student_kernel(x_ref, o_ref, wq_ref, wk_ref, gq_ref, gk_ref, fq_s, fk_s, st_s):
    total = x_ref.shape[0]
    count = total // CHUNK
    sl = [slice(c * CHUNK, (c + 1) * CHUNK) for c in range(count)]
    wq, wk = signed_pair(wq_ref[...]), signed_pair(wk_ref[...])
    one = jnp.ones((CHUNK, 128), bf16)

    def values_and_ones(c):
        return lanes(x_ref[sl[c], 2 * HD :], one)

    state = jnp.zeros((2 * FEAT, 256), f32)
    for g in range(0, count, TOGETHER):
        cs = range(g, min(g + TOGETHER, count))
        lq = [dot(lanes(x_ref[sl[c], :HD], x_ref[sl[c], :HD]), wq) for c in cs]
        lk = [dot(lanes(*[x_ref[sl[c], HD : 2 * HD]] * 2), wk) for c in cs]
        fk = [phi(x) for x in lk]
        fq = [phi(x) for x in lq]
        add = [dot(f.astype(bf16), values_and_ones(c), TN) for f, c in zip(fk, cs)]
        for i, c in enumerate(cs):
            fq_s[sl[c], :] = fq[i]
            fk_s[sl[c], :] = fk[i]
            st_s[c] = state.astype(bf16)
            state = state + add[i]

    r = lax.broadcasted_iota(jnp.int32, (CHUNK, CHUNK), 0)
    k = lax.broadcasted_iota(jnp.int32, (CHUNK, CHUNK), 1)
    later = jnp.zeros((2 * FEAT, 256), f32)
    gq = jnp.zeros((HD, 256), f32)
    gk = jnp.zeros((HD, 256), f32)
    for g in reversed(range(0, count, TOGETHER)):
        cs = list(reversed(range(g, min(g + TOGETHER, count))))
        every = range(len(cs))
        ve = [values_and_ones(c) for c in cs]
        st = [st_s[c] for c in cs]
        fq = [split(fq_s[sl[c], :]) for c in cs]
        fk = [split(fk_s[sl[c], :]) for c in cs]
        at = []
        for i in every:
            a = dot(fq[i][0], fk[i][0], NT)
            if cs[i] == 0:
                a = a + dot(lanes(*fq[i]), lanes(fk[i][1], fk[i][0]), NT)
            at.append(split(jnp.where(r >= k, a, 0.0)))
        nd = [dot(lanes(*at[i], fq[i][0]), rows(ve[i], ve[i], st[i])) for i in every]
        inv = [1.0 / x[:, HD:] for x in nd]
        out = [x[:, :HD] * y for x, y in zip(nd, inv)]
        dn = [(out[i] - o_ref[sl[cs[i]], :].astype(f32)) * inv[i] * (2.0 / total) for i in every]
        dd = [split(jnp.sum(dn[i] * out[i], axis=1, keepdims=True) * (-1.0 / 64)) for i in every]
        dd = [jnp.where(first_half((CHUNK, 128)), h.astype(f32), l.astype(f32)).astype(bf16) for h, l in dd]
        dx = [lanes(dn[i].astype(bf16), dd[i]) for i in every]
        da, dat = [], []
        for i in every:
            a, b = dot(dx[i], ve[i], NT), dot(ve[i], dx[i], NT)
            if cs[i] == 0:
                low = split(dn[i])[1]
                a, b = a + dot(low, ve[i][:, :HD], NT), b + dot(ve[i][:, :HD], low, NT)
            da.append(split(jnp.where(r >= k, a, 0.0)))
            dat.append(split(jnp.where(r <= k, b, 0.0)))
        after = []
        for i in every:
            after.append(later.astype(bf16))
            later = later + dot(fq[i][0], dx[i], TN)
        x = [dot(da[i][0], lanes(*fk[i])) for i in every]
        dfq = [x[i][:, :128] + x[i][:, 128:] + dot(da[i][1], fk[i][0]) + dot(dx[i], st[i], NT) for i in every]
        x = [dot(dat[i][0], lanes(*fq[i])) for i in every]
        dfk = [x[i][:, :128] + x[i][:, 128:] + dot(dat[i][1], fq[i][0]) + dot(ve[i], after[i], NT) for i in every]
        yq = [lanes(*split(phi_back(fq_s[sl[cs[i]], :], dfq[i]))) for i in every]
        yk = [lanes(*split(phi_back(fk_s[sl[cs[i]], :], dfk[i]))) for i in every]
        lo, hi = sl[cs[-1]].start, sl[cs[0]].stop
        gq = gq + dot(x_ref[lo:hi, :HD], rows(*yq[::-1]), TN)
        gk = gk + dot(x_ref[lo:hi, HD : 2 * HD], rows(*yk[::-1]), TN)

    def fold(g):
        g = g[:, :128] + g[:, 128:]
        return g[:, :FEAT] - g[:, FEAT:]

    gq_ref[...] = fold(gq)
    gk_ref[...] = fold(gk)


def student(x, o, wq, wk):
    total = x.shape[0]
    return pl.pallas_call(
        student_kernel,
        out_shape=[jax.ShapeDtypeStruct(wq.shape, f32)] * 2,
        scratch_shapes=[
            pltpu.VMEM((total, 2 * FEAT), f32),
            pltpu.VMEM((total, 2 * FEAT), f32),
            pltpu.VMEM((total // CHUNK, 2 * FEAT, 256), bf16),
        ],
        compiler_params=pltpu.CompilerParams(vmem_limit_bytes=56 << 20),
        name="student",
    )(x, o, wq, wk)


def shards(queries, keys, values, query_map, key_map):
    tok = queries.shape[0]
    peers = lax.axis_size("seq")
    mine = lax.axis_index("seq")
    kv = jnp.broadcast_to(lanes(keys, values)[None], (peers, tok, 2 * HD))
    qs = queries.reshape(tok, peers, HD).transpose(1, 0, 2)
    x = lax.all_to_all(jnp.concatenate([qs, kv], axis=2), "seq", 0, 0, tiled=True)
    x = x.reshape(peers * tok, 3 * HD)
    wq = lax.dynamic_index_in_dim(query_map, mine, 0, keepdims=False)
    wk = lax.dynamic_index_in_dim(key_map, mine, 0, keepdims=False)
    gq, gk = student(x, teacher(x), wq, wk)
    return gq[None], gk[None]


def solution(mesh):
    return jax.shard_map(
        shards,
        mesh=mesh,
        in_specs=(
            P("seq", "kv"),
            P("seq", "kv"),
            P("seq", "kv"),
            P("kv", None, None),
            P("kv", None, None),
        ),
        out_specs=(P(("kv", "seq"), None, None), P(("kv", "seq"), None, None)),
        check_vma=False,
    )
```

```python
import functools

import jax
import jax.numpy as jnp
from jax import lax
from jax.experimental import pallas as pl
from jax.experimental.pallas import tpu as pltpu
from jax.sharding import PartitionSpec as P

f32, bf16 = jnp.float32, jnp.bfloat16
HD = 128
FEAT = 64
CHUNK = 256
TOGETHER = 8
NT = (((1,), (1,)), ((), ()))
NN = (((1,), (0,)), ((), ()))
TN = (((0,), (0,)), ((), ()))


def dot(a, b, dims=NN):
    return lax.dot_general(a, b, dims, preferred_element_type=f32)


def lanes(*xs):
    return jnp.concatenate(xs, axis=1)


def rows(*xs):
    return jnp.concatenate(xs, axis=0)


def split(x):
    high = x.astype(bf16)
    return high, (x - high.astype(f32)).astype(bf16)


def first_half(shape):
    return lax.broadcasted_iota(jnp.int32, shape, 1) < FEAT


def half_sums(x):
    lo = first_half(x.shape)
    a = jnp.sum(jnp.where(lo, x, 0.0), axis=1, keepdims=True)
    b = jnp.sum(jnp.where(lo, 0.0, x), axis=1, keepdims=True)
    return a, b


def phi(logits):
    lo = first_half(logits.shape)
    a = jnp.max(jnp.where(lo, logits, -jnp.inf), axis=1, keepdims=True)
    b = jnp.max(jnp.where(lo, -jnp.inf, logits), axis=1, keepdims=True)
    e = jnp.exp(logits - jnp.where(lo, a, b))
    a, b = half_sums(e)
    return e * jnp.where(lo, 1.0 / a, 1.0 / b)


def phi_back(p, d):
    x = p * d
    a, b = half_sums(x)
    return x - p * jnp.where(first_half(x.shape), a, b)


def lane_max(s):
    m = s[:, :128]
    for at in range(128, s.shape[1], 128):
        m = jnp.maximum(m, s[:, at : at + 128])
    return m


def teach(q_ref, kv_ref, o_ref, score, block):
    total = q_ref.shape[0]
    exponent = 1.4426950408889634 / HD**0.5

    def scores(i):
        q = q_ref[i * block : (i + 1) * block, :]
        peak = None
        for j in range(i + 1):
            s = dot(q, kv_ref[j * block : (j + 1) * block, :HD], NT)
            if j == i:
                r = lax.broadcasted_iota(jnp.int32, s.shape, 0)
                c = lax.broadcasted_iota(jnp.int32, s.shape, 1)
                s = jnp.where(r >= c, s, -1e30)
            score[i % 2, :, j * block : (j + 1) * block] = s
            m = lane_max(s)
            peak = m if peak is None else jnp.maximum(peak, m)
        return jnp.max(peak, axis=1, keepdims=True)

    def mix(i, peak):
        n = (i + 1) * block
        ve = lanes(kv_ref[:n, HD:], jnp.ones((n, 128), bf16))
        shift = peak * exponent
        p = [
            jnp.exp2(score[i % 2, :, j * block : (j + 1) * block] * exponent - shift)
            for j in range(i + 1)
        ]
        if i == 0:
            high, low = split(p[0])
            acc = dot(lanes(high, low), rows(ve, ve))
        else:
            acc = dot(lanes(*(x.astype(bf16) for x in p)), ve)
        o_ref[i * block : (i + 1) * block, :] = (acc[:, :HD] / acc[:, HD:]).astype(bf16)

    peak = scores(0)
    for i in range(total // block):
        following = scores(i + 1) if (i + 1) * block < total else None
        mix(i, peak)
        peak = following


def signed_pair(w):
    return lanes(*split(rows(w, -w)))


def whole(a):
    return pl.BlockSpec(a.shape, lambda i, m: (0,) * len(a.shape))


def head_block(w):
    return pl.BlockSpec((1,) + w.shape[1:], lambda i, m: (m[0], 0, 0))


def learn(q_ref, kv_ref, o_ref, fq_s, fk_s, st_s, gq_ref, gk_ref):
    total = q_ref.shape[0]
    count = total // CHUNK
    sl = [slice(c * CHUNK, (c + 1) * CHUNK) for c in range(count)]
    one = jnp.ones((CHUNK, 128), bf16)

    def values_and_ones(c):
        return lanes(kv_ref[sl[c], HD:], one)

    r = lax.broadcasted_iota(jnp.int32, (CHUNK, CHUNK), 0)
    k = lax.broadcasted_iota(jnp.int32, (CHUNK, CHUNK), 1)
    later = jnp.zeros((2 * FEAT, 256), f32)
    gq = jnp.zeros((HD, 256), f32)
    gk = jnp.zeros((HD, 256), f32)
    for g in reversed(range(0, count, TOGETHER)):
        cs = list(reversed(range(g, min(g + TOGETHER, count))))
        every = range(len(cs))
        ve = [values_and_ones(c) for c in cs]
        st = [st_s[c] for c in cs]
        fq = [split(fq_s[sl[c], :]) for c in cs]
        fk = [split(fk_s[sl[c], :]) for c in cs]
        at = []
        for i in every:
            a = dot(fq[i][0], fk[i][0], NT)
            if cs[i] == 0:
                a = a + dot(lanes(*fq[i]), lanes(fk[i][1], fk[i][0]), NT)
            at.append(split(jnp.where(r >= k, a, 0.0)))
        nd = [dot(lanes(*at[i], fq[i][0]), rows(ve[i], ve[i], st[i])) for i in every]
        inv = [1.0 / x[:, HD:] for x in nd]
        out = [x[:, :HD] * y for x, y in zip(nd, inv)]
        dn = [(out[i] - o_ref[sl[cs[i]], :].astype(f32)) * inv[i] * (2.0 / total) for i in every]
        dd = [split(jnp.sum(dn[i] * out[i], axis=1, keepdims=True) * (-1.0 / 64)) for i in every]
        dd = [jnp.where(first_half((CHUNK, 128)), h.astype(f32), l.astype(f32)).astype(bf16) for h, l in dd]
        dx = [lanes(dn[i].astype(bf16), dd[i]) for i in every]
        da, dat = [], []
        for i in every:
            a, b = dot(dx[i], ve[i], NT), dot(ve[i], dx[i], NT)
            if cs[i] == 0:
                low = split(dn[i])[1]
                a, b = a + dot(low, ve[i][:, :HD], NT), b + dot(ve[i][:, :HD], low, NT)
            da.append(split(jnp.where(r >= k, a, 0.0)))
            dat.append(split(jnp.where(r <= k, b, 0.0)))
        after = []
        for i in every:
            after.append(later.astype(bf16))
            later = later + dot(fq[i][0], dx[i], TN)
        x = [dot(da[i][0], lanes(*fk[i])) for i in every]
        dfq = [x[i][:, :128] + x[i][:, 128:] + dot(da[i][1], fk[i][0]) + dot(dx[i], st[i], NT) for i in every]
        x = [dot(dat[i][0], lanes(*fq[i])) for i in every]
        dfk = [x[i][:, :128] + x[i][:, 128:] + dot(dat[i][1], fq[i][0]) + dot(ve[i], after[i], NT) for i in every]
        yq = [lanes(*split(phi_back(fq_s[sl[cs[i]], :], dfq[i]))) for i in every]
        yk = [lanes(*split(phi_back(fk_s[sl[cs[i]], :], dfk[i]))) for i in every]
        lo, hi = sl[cs[-1]].start, sl[cs[0]].stop
        gq = gq + dot(q_ref[lo:hi, :], rows(*yq[::-1]), TN)
        gk = gk + dot(kv_ref[lo:hi, :HD], rows(*yk[::-1]), TN)

    def fold(g):
        g = g[:, :128] + g[:, 128:]
        return g.T[:FEAT] - g.T[FEAT:]

    gq_ref[...] = fold(gq)
    gk_ref[...] = fold(gk)


def features(q_ref, kv_ref, wq, wk, fq_s, fk_s, st_s):
    one = jnp.ones((CHUNK, 128), bf16)
    state = jnp.zeros((2 * FEAT, 256), f32)
    count = q_ref.shape[0] // CHUNK
    sl = [slice(c * CHUNK, (c + 1) * CHUNK) for c in range(count)]
    for g in range(0, count, TOGETHER):
        cs = range(g, min(g + TOGETHER, count))
        lq = [dot(lanes(*[q_ref[sl[c], :]] * 2), wq, NT) for c in cs]
        lk = [dot(lanes(*[kv_ref[sl[c], :HD]] * 2), wk, NT) for c in cs]
        fk = [phi(x) for x in lk]
        fq = [phi(x) for x in lq]
        add = [dot(f.astype(bf16), lanes(kv_ref[sl[c], HD:], one), TN) for f, c in zip(fk, cs)]
        for i, c in enumerate(cs):
            fq_s[sl[c], :] = fq[i]
            fk_s[sl[c], :] = fk[i]
            st_s[c] = state.astype(bf16)
            state = state + add[i]


def assemble(mine, pieces, kv_ref):
    tok = pieces[0].shape[1]
    y, core = mine // 4, mine % 2
    spans = len(pieces) // 2
    for side in range(2):
        c = core if side == 0 else 1 - core
        for d in range(spans):
            from_y = (y + spans - d) % spans
            for z in range(2):
                at = pl.multiple_of((from_y * 4 + z * 2 + c) * tok, tok)
                kv_ref[pl.ds(at, tok), :] = pieces[side * spans + d][z]


def layer_kernel(mine_ref, q_ref, *refs):
    *pieces, wq_ref, wk_ref, gq_ref, gk_ref, kv_s, o_s, score, fq_s, fk_s, st_s = refs
    assemble(mine_ref[0], pieces, kv_s)
    features(q_ref, kv_s, signed_pair(wq_ref[0]), signed_pair(wk_ref[0]), fq_s, fk_s, st_s)
    teach(q_ref, kv_s, o_s, score, CHUNK)
    learn(q_ref, kv_s, o_s, fq_s, fk_s, st_s, gq_ref, gk_ref)


def layer(mine, q, pieces, wq, wk):
    total = q.shape[0]
    out = [jax.ShapeDtypeStruct((FEAT, HD), f32)] * 2
    return pl.pallas_call(
        layer_kernel,
        grid_spec=pltpu.PrefetchScalarGridSpec(
            num_scalar_prefetch=1,
            grid=(1,),
            in_specs=[whole(q)] + [whole(a) for a in pieces] + [head_block(wq), head_block(wk)],
            out_specs=[whole(o) for o in out],
            scratch_shapes=[
                pltpu.VMEM((total, 2 * HD), bf16),
                pltpu.VMEM((total, HD), bf16),
                pltpu.VMEM((2, CHUNK, total), f32),
                pltpu.VMEM((total, 2 * FEAT), f32),
                pltpu.VMEM((total, 2 * FEAT), f32),
                pltpu.VMEM((total // CHUNK, 2 * FEAT, 256), bf16),
            ],
        ),
        out_shape=out,
        compiler_params=pltpu.CompilerParams(vmem_limit_bytes=56 << 20),
        name="layer",
    )(mine, q, *pieces, wq, wk)


def step(x, move):
    return lax.ppermute(x, "seq", [(i, move(i)) for i in range(lax.axis_size("seq"))])


def shards(queries, keys, values, query_map, key_map):
    tok = queries.shape[0]
    peers = lax.axis_size("seq")
    mine = lax.axis_index("seq")
    here = lanes(keys, values)
    over = step(here, lambda i: i ^ 2)
    low = mine // 2 % 2 == 0
    pair = jnp.stack([jnp.where(low, here, over), jnp.where(low, over, here)])
    up = lambda x: step(x, lambda i: (i + 4) % peers)
    down = lambda x: step(x, lambda i: (i - 4) % peers)
    pieces = [pair] + [step(pair, lambda i, d=d: (i + 4 * d) % peers) for d in range(1, peers // 4)]
    pieces = pieces + [step(x, lambda i: i ^ 1) for x in pieces]
    qs = queries.reshape(tok, peers, HD).transpose(1, 0, 2)
    q = lax.all_to_all(qs, "seq", 0, 0, tiled=True).reshape(peers * tok, HD)
    gq, gk = layer(
        mine.astype(jnp.int32).reshape(1),
        q,
        pieces,
        query_map.transpose(0, 2, 1),
        key_map.transpose(0, 2, 1),
    )
    return gq.T[None], gk.T[None]


def solution(mesh):
    return jax.shard_map(
        shards,
        mesh=mesh,
        in_specs=(
            P("seq", "kv"),
            P("seq", "kv"),
            P("seq", "kv"),
            P("kv", None, None),
            P("kv", None, None),
        ),
        out_specs=(P(("kv", "seq"), None, None), P(("kv", "seq"), None, None)),
        check_vma=False,
    )
```

```python
import functools

import jax
import jax.numpy as jnp
from jax import lax
from jax.experimental import pallas as pl
from jax.experimental.pallas import tpu as pltpu
from jax.sharding import PartitionSpec as P

f32, bf16 = jnp.float32, jnp.bfloat16
HD = 128
FEAT = 64
CHUNK = 256
TOGETHER = 8
NT = (((1,), (1,)), ((), ()))
NN = (((1,), (0,)), ((), ()))
TN = (((0,), (0,)), ((), ()))


def dot(a, b, dims=NN):
    return lax.dot_general(a, b, dims, preferred_element_type=f32)


def lanes(*xs):
    return jnp.concatenate(xs, axis=1)


def rows(*xs):
    return jnp.concatenate(xs, axis=0)


def split(x):
    high = x.astype(bf16)
    return high, (x - high.astype(f32)).astype(bf16)


def first_half(shape):
    return lax.broadcasted_iota(jnp.int32, shape, 1) < FEAT


def half_sums(x):
    lo = first_half(x.shape)
    a = jnp.sum(jnp.where(lo, x, 0.0), axis=1, keepdims=True)
    b = jnp.sum(jnp.where(lo, 0.0, x), axis=1, keepdims=True)
    return a, b


def phi(logits):
    lo = first_half(logits.shape)
    a = jnp.max(jnp.where(lo, logits, -jnp.inf), axis=1, keepdims=True)
    b = jnp.max(jnp.where(lo, -jnp.inf, logits), axis=1, keepdims=True)
    e = jnp.exp(logits - jnp.where(lo, a, b))
    a, b = half_sums(e)
    return e * jnp.where(lo, 1.0 / a, 1.0 / b)


def phi_back(p, d):
    x = p * d
    a, b = half_sums(x)
    return x - p * jnp.where(first_half(x.shape), a, b)


def lane_max(s):
    m = s[:, :128]
    for at in range(128, s.shape[1], 128):
        m = jnp.maximum(m, s[:, at : at + 128])
    return m


def teach(q_ref, kv_ref, o_ref, score, block):
    total = q_ref.shape[0]
    exponent = 1.4426950408889634 / HD**0.5

    def scores(i):
        q = q_ref[i * block : (i + 1) * block, :]
        peak = None
        for j in range(i + 1):
            s = dot(q, kv_ref[j * block : (j + 1) * block, :HD], NT)
            if j == i:
                r = lax.broadcasted_iota(jnp.int32, s.shape, 0)
                c = lax.broadcasted_iota(jnp.int32, s.shape, 1)
                s = jnp.where(r >= c, s, -1e30)
            score[i % 2, :, j * block : (j + 1) * block] = s
            m = lane_max(s)
            peak = m if peak is None else jnp.maximum(peak, m)
        return jnp.max(peak, axis=1, keepdims=True)

    def mix(i, peak):
        n = (i + 1) * block
        ve = lanes(kv_ref[:n, HD:], jnp.ones((n, 128), bf16))
        shift = peak * exponent
        p = [
            jnp.exp2(score[i % 2, :, j * block : (j + 1) * block] * exponent - shift)
            for j in range(i + 1)
        ]
        if i == 0:
            high, low = split(p[0])
            acc = dot(lanes(high, low), rows(ve, ve))
        else:
            acc = dot(lanes(*(x.astype(bf16) for x in p)), ve)
        o_ref[i * block : (i + 1) * block, :] = (acc[:, :HD] / acc[:, HD:]).astype(bf16)

    peak = scores(0)
    for i in range(total // block):
        following = scores(i + 1) if (i + 1) * block < total else None
        mix(i, peak)
        peak = following


def signed_pair(w):
    return lanes(*split(rows(w, -w)))


def whole(a):
    return pl.BlockSpec(a.shape, lambda i, m: (0,) * len(a.shape))


def head_block(w):
    return pl.BlockSpec((1,) + w.shape[1:], lambda i, m: (m[0], 0, 0))


def learn(q_ref, kv_ref, o_ref, fq_s, fk_s, st_s, gq_ref, gk_ref):
    total = q_ref.shape[0]
    count = total // CHUNK
    sl = [slice(c * CHUNK, (c + 1) * CHUNK) for c in range(count)]
    one = jnp.ones((CHUNK, 128), bf16)

    def values_and_ones(c):
        return lanes(kv_ref[sl[c], HD:], one)

    r = lax.broadcasted_iota(jnp.int32, (CHUNK, CHUNK), 0)
    k = lax.broadcasted_iota(jnp.int32, (CHUNK, CHUNK), 1)
    later = jnp.zeros((2 * FEAT, 256), f32)
    gq = jnp.zeros((HD, 256), f32)
    gk = jnp.zeros((HD, 256), f32)
    for g in reversed(range(0, count, TOGETHER)):
        cs = list(reversed(range(g, min(g + TOGETHER, count))))
        every = range(len(cs))
        ve = [values_and_ones(c) for c in cs]
        st = [st_s[c] for c in cs]
        fq = [split(fq_s[sl[c], :]) for c in cs]
        fk = [split(fk_s[sl[c], :]) for c in cs]
        at = []
        for i in every:
            a = dot(fq[i][0], fk[i][0], NT)
            if cs[i] == 0:
                a = a + dot(lanes(*fq[i]), lanes(fk[i][1], fk[i][0]), NT)
            at.append(split(jnp.where(r >= k, a, 0.0)))
        nd = [dot(lanes(*at[i], fq[i][0]), rows(ve[i], ve[i], st[i])) for i in every]
        inv = [1.0 / x[:, HD:] for x in nd]
        out = [x[:, :HD] * y for x, y in zip(nd, inv)]
        dn = [(out[i] - o_ref[sl[cs[i]], :].astype(f32)) * inv[i] * (2.0 / total) for i in every]
        dd = [split(jnp.sum(dn[i] * out[i], axis=1, keepdims=True) * (-1.0 / 64)) for i in every]
        dd = [jnp.where(first_half((CHUNK, 128)), h.astype(f32), l.astype(f32)).astype(bf16) for h, l in dd]
        dx = [lanes(dn[i].astype(bf16), dd[i]) for i in every]
        da, dat = [], []
        for i in every:
            a, b = dot(dx[i], ve[i], NT), dot(ve[i], dx[i], NT)
            if cs[i] == 0:
                low = split(dn[i])[1]
                a, b = a + dot(low, ve[i][:, :HD], NT), b + dot(ve[i][:, :HD], low, NT)
            da.append(split(jnp.where(r >= k, a, 0.0)))
            dat.append(split(jnp.where(r <= k, b, 0.0)))
        after = []
        for i in every:
            after.append(later.astype(bf16))
            later = later + dot(fq[i][0], dx[i], TN)
        x = [dot(da[i][0], lanes(*fk[i])) for i in every]
        dfq = [x[i][:, :128] + x[i][:, 128:] + dot(da[i][1], fk[i][0]) + dot(dx[i], st[i], NT) for i in every]
        x = [dot(dat[i][0], lanes(*fq[i])) for i in every]
        dfk = [x[i][:, :128] + x[i][:, 128:] + dot(dat[i][1], fq[i][0]) + dot(ve[i], after[i], NT) for i in every]
        yq = [lanes(*split(phi_back(fq_s[sl[cs[i]], :], dfq[i]))) for i in every]
        yk = [lanes(*split(phi_back(fk_s[sl[cs[i]], :], dfk[i]))) for i in every]
        lo, hi = sl[cs[-1]].start, sl[cs[0]].stop
        gq = gq + dot(q_ref[lo:hi, :], rows(*yq[::-1]), TN)
        gk = gk + dot(kv_ref[lo:hi, :HD], rows(*yk[::-1]), TN)

    def fold(g):
        g = g[:, :128] + g[:, 128:]
        return g.T[:FEAT] - g.T[FEAT:]

    gq_ref[...] = fold(gq)
    gk_ref[...] = fold(gk)


def query_features_kernel(mine_ref, q_ref, w_ref, f_ref):
    w = signed_pair(w_ref[0])
    sl = [slice(at, at + CHUNK) for at in range(0, q_ref.shape[0], CHUNK)]
    for g in range(0, len(sl), TOGETHER):
        group = sl[g : g + TOGETHER]
        logits = [dot(lanes(*[q_ref[x, :]] * 2), w, NT) for x in group]
        fq = [phi(x) for x in logits]
        for x, f in zip(group, fq):
            f_ref[x, :] = f


IN_VMEM = pl.BlockSpec(memory_space=pltpu.VMEM)


def in_vmem(x):
    return pltpu.with_memory_space_constraint(x, pltpu.VMEM)


def query_features(mine, q, w):
    return pl.pallas_call(
        query_features_kernel,
        grid_spec=pltpu.PrefetchScalarGridSpec(
            num_scalar_prefetch=1,
            grid=(1,),
            in_specs=[IN_VMEM, head_block(w)],
            out_specs=IN_VMEM,
        ),
        out_shape=jax.ShapeDtypeStruct((q.shape[0], 2 * FEAT), f32),
        compiler_params=pltpu.CompilerParams(vmem_limit_bytes=48 << 20),
        name="query_features",
    )(mine, in_vmem(q), w)


def key_features(kv_ref, wk, fk_s, st_s):
    one = jnp.ones((CHUNK, 128), bf16)
    state = jnp.zeros((2 * FEAT, 256), f32)
    count = kv_ref.shape[0] // CHUNK
    sl = [slice(c * CHUNK, (c + 1) * CHUNK) for c in range(count)]
    for g in range(0, count, TOGETHER):
        cs = range(g, min(g + TOGETHER, count))
        lk = [dot(lanes(*[kv_ref[sl[c], :HD]] * 2), wk, NT) for c in cs]
        fk = [phi(x) for x in lk]
        add = [dot(f.astype(bf16), lanes(kv_ref[sl[c], HD:], one), TN) for f, c in zip(fk, cs)]
        for i, c in enumerate(cs):
            fk_s[sl[c], :] = fk[i]
            st_s[c] = state.astype(bf16)
            state = state + add[i]


def assemble(mine, pieces, kv_ref):
    tok = pieces[0].shape[0]
    y, z, core = mine // 4, mine // 2 % 2, mine % 2
    spans = len(pieces) // 4
    for n, piece in enumerate(pieces):
        side, d = divmod(n, spans)
        from_y = (y + spans - d) % spans
        from_z = z if side % 2 == 0 else 1 - z
        from_core = core if side < 2 else 1 - core
        at = pl.multiple_of((from_y * 4 + from_z * 2 + from_core) * tok, tok)
        kv_ref[pl.ds(at, tok), :] = piece[...]


def layer_kernel(mine_ref, q_ref, fq_s, *refs):
    *pieces, wk_ref, gq_ref, gk_ref, kv_s, o_s, score, fk_s, st_s = refs
    assemble(mine_ref[0], pieces, kv_s)
    key_features(kv_s, signed_pair(wk_ref[0]), fk_s, st_s)
    teach(q_ref, kv_s, o_s, score, CHUNK)
    learn(q_ref, kv_s, o_s, fq_s, fk_s, st_s, gq_ref, gk_ref)


def layer(mine, q, fq, pieces, wk):
    total = q.shape[0]
    out = [jax.ShapeDtypeStruct((FEAT, HD), f32)] * 2
    return pl.pallas_call(
        layer_kernel,
        grid_spec=pltpu.PrefetchScalarGridSpec(
            num_scalar_prefetch=1,
            grid=(1,),
            in_specs=[IN_VMEM] * (2 + len(pieces)) + [head_block(wk)],
            out_specs=[whole(o) for o in out],
            scratch_shapes=[
                pltpu.VMEM((total, 2 * HD), bf16),
                pltpu.VMEM((total, HD), bf16),
                pltpu.VMEM((2, CHUNK, total), f32),
                pltpu.VMEM((total, 2 * FEAT), f32),
                pltpu.VMEM((total // CHUNK, 2 * FEAT, 256), bf16),
            ],
        ),
        out_shape=out,
        compiler_params=pltpu.CompilerParams(vmem_limit_bytes=48 << 20),
        name="layer",
    )(mine, *(in_vmem(a) for a in (q, fq, *pieces)), wk)


def step(x, move):
    return lax.ppermute(x, "seq", [(i, move(i)) for i in range(lax.axis_size("seq"))])


def shards(queries, keys, values, query_map, key_map):
    tok = queries.shape[0]
    peers = lax.axis_size("seq")
    mine = lax.axis_index("seq")
    here = lanes(keys, values)
    pieces = [here] + [step(here, lambda i, d=d: (i + 4 * d) % peers) for d in range(1, peers // 4)]
    over = [step(x, lambda i: i ^ 2) for x in pieces]
    qs = queries.reshape(tok, peers, HD).transpose(1, 0, 2)
    q = lax.all_to_all(qs, "seq", 0, 0, tiled=True).reshape(peers * tok, HD)
    index = mine.astype(jnp.int32).reshape(1)
    fq = query_features(index, q, query_map.transpose(0, 2, 1))
    fq, over[-1] = lax.optimization_barrier((fq, over[-1]))
    pieces = pieces + over
    pieces = pieces + [step(x, lambda i: i ^ 1) for x in pieces]
    gq, gk = layer(index, q, fq, pieces, key_map.transpose(0, 2, 1))
    return gq.T[None], gk.T[None]


def solution(mesh):
    return jax.shard_map(
        shards,
        mesh=mesh,
        in_specs=(
            P("seq", "kv"),
            P("seq", "kv"),
            P("seq", "kv"),
            P("kv", None, None),
            P("kv", None, None),
        ),
        out_specs=(P(("kv", "seq"), None, None), P(("kv", "seq"), None, None)),
        check_vma=False,
    )
```

```python
import functools

import jax
import jax.numpy as jnp
from jax import lax
from jax.experimental import pallas as pl
from jax.experimental.pallas import tpu as pltpu
from jax.sharding import PartitionSpec as P

f32, bf16 = jnp.float32, jnp.bfloat16
HD = 128
FEAT = 64
CHUNK = 256
TOGETHER = 8
NT = (((1,), (1,)), ((), ()))
NN = (((1,), (0,)), ((), ()))
TN = (((0,), (0,)), ((), ()))


def dot(a, b, dims=NN):
    return lax.dot_general(a, b, dims, preferred_element_type=f32)


def lanes(*xs):
    return jnp.concatenate(xs, axis=1)


def rows(*xs):
    return jnp.concatenate(xs, axis=0)


def split(x):
    high = x.astype(bf16)
    return high, (x - high.astype(f32)).astype(bf16)


def first_half(shape):
    return lax.broadcasted_iota(jnp.int32, shape, 1) < FEAT


def half_sums(x):
    lo = first_half(x.shape)
    a = jnp.sum(jnp.where(lo, x, 0.0), axis=1, keepdims=True)
    b = jnp.sum(jnp.where(lo, 0.0, x), axis=1, keepdims=True)
    return a, b


def phi(logits):
    lo = first_half(logits.shape)
    a = jnp.max(jnp.where(lo, logits, -jnp.inf), axis=1, keepdims=True)
    b = jnp.max(jnp.where(lo, -jnp.inf, logits), axis=1, keepdims=True)
    e = jnp.exp(logits - jnp.where(lo, a, b))
    a, b = half_sums(e)
    return e * jnp.where(lo, 1.0 / a, 1.0 / b)


def phi_back(p, d):
    x = p * d
    a, b = half_sums(x)
    return x - p * jnp.where(first_half(x.shape), a, b)


def lane_max(s):
    m = s[:, :128]
    for at in range(128, s.shape[1], 128):
        m = jnp.maximum(m, s[:, at : at + 128])
    return m


def teach(q_ref, kv_ref, o_ref, score, block):
    total = q_ref.shape[0]
    exponent = 1.4426950408889634 / HD**0.5

    def scores(i):
        q = q_ref[i * block : (i + 1) * block, :]
        peak = None
        for j in range(i + 1):
            s = dot(q, kv_ref[j * block : (j + 1) * block, :HD], NT)
            if j == i:
                r = lax.broadcasted_iota(jnp.int32, s.shape, 0)
                c = lax.broadcasted_iota(jnp.int32, s.shape, 1)
                s = jnp.where(r >= c, s, -1e30)
            score[i % 2, :, j * block : (j + 1) * block] = s
            m = lane_max(s)
            peak = m if peak is None else jnp.maximum(peak, m)
        return jnp.max(peak, axis=1, keepdims=True)

    def mix(i, peak):
        n = (i + 1) * block
        ve = lanes(kv_ref[:n, HD:], jnp.ones((n, 128), bf16))
        shift = peak * exponent
        p = [
            jnp.exp2(score[i % 2, :, j * block : (j + 1) * block] * exponent - shift)
            for j in range(i + 1)
        ]
        if i == 0:
            high, low = split(p[0])
            acc = dot(lanes(high, low), rows(ve, ve))
        else:
            acc = dot(lanes(*(x.astype(bf16) for x in p)), ve)
        o_ref[i * block : (i + 1) * block, :] = (acc[:, :HD] / acc[:, HD:]).astype(bf16)

    peak = scores(0)
    for i in range(total // block):
        following = scores(i + 1) if (i + 1) * block < total else None
        mix(i, peak)
        peak = following


def signed_pair(w):
    return lanes(*split(rows(w, -w)))


def whole(a):
    return pl.BlockSpec(a.shape, lambda i, m: (0,) * len(a.shape))


def head_block(w):
    return pl.BlockSpec((1,) + w.shape[1:], lambda i, m: (m[0], 0, 0))


def learn(q_ref, kv_ref, o_ref, fq_s, fk_s, st_s, gq_ref, gk_ref):
    total = q_ref.shape[0]
    count = total // CHUNK
    sl = [slice(c * CHUNK, (c + 1) * CHUNK) for c in range(count)]
    one = jnp.ones((CHUNK, 128), bf16)

    def values_and_ones(c):
        return lanes(kv_ref[sl[c], HD:], one)

    r = lax.broadcasted_iota(jnp.int32, (CHUNK, CHUNK), 0)
    k = lax.broadcasted_iota(jnp.int32, (CHUNK, CHUNK), 1)
    later = jnp.zeros((2 * FEAT, 256), f32)
    gq = jnp.zeros((HD, 256), f32)
    gk = jnp.zeros((HD, 256), f32)
    for g in reversed(range(0, count, TOGETHER)):
        cs = list(reversed(range(g, min(g + TOGETHER, count))))
        every = range(len(cs))
        ve = [values_and_ones(c) for c in cs]
        st = [st_s[c] for c in cs]
        fq = [split(fq_s[sl[c], :]) for c in cs]
        fk = [split(fk_s[sl[c], :]) for c in cs]
        at = []
        for i in every:
            a = dot(fq[i][0], fk[i][0], NT)
            if cs[i] == 0:
                a = a + dot(lanes(*fq[i]), lanes(fk[i][1], fk[i][0]), NT)
            at.append(split(jnp.where(r >= k, a, 0.0)))
        nd = [dot(lanes(*at[i], fq[i][0]), rows(ve[i], ve[i], st[i])) for i in every]
        inv = [1.0 / x[:, HD:] for x in nd]
        out = [x[:, :HD] * y for x, y in zip(nd, inv)]
        dn = [(out[i] - o_ref[sl[cs[i]], :].astype(f32)) * inv[i] * (2.0 / total) for i in every]
        dd = [split(jnp.sum(dn[i] * out[i], axis=1, keepdims=True) * (-1.0 / 64)) for i in every]
        dd = [jnp.where(first_half((CHUNK, 128)), h.astype(f32), l.astype(f32)).astype(bf16) for h, l in dd]
        dx = [lanes(dn[i].astype(bf16), dd[i]) for i in every]
        da = []
        for i in every:
            a = dot(dx[i], ve[i], NT)
            if cs[i] == 0:
                a = a + dot(split(dn[i])[1], ve[i][:, :HD], NT)
            da.append(split(jnp.where(r >= k, a, 0.0)))
        after = []
        for i in every:
            after.append(later.astype(bf16))
            later = later + dot(fq[i][0], dx[i], TN)
        x = [dot(da[i][0], lanes(*fk[i])) for i in every]
        dfq = [x[i][:, :128] + x[i][:, 128:] + dot(da[i][1], fk[i][0]) + dot(dx[i], st[i], NT) for i in every]
        x = [dot(da[i][0], lanes(*fq[i]), TN) for i in every]
        dfk = [x[i][:, :128] + x[i][:, 128:] + dot(da[i][1], fq[i][0], TN) + dot(ve[i], after[i], NT) for i in every]
        yq = [lanes(*split(phi_back(fq_s[sl[cs[i]], :], dfq[i]))) for i in every]
        yk = [lanes(*split(phi_back(fk_s[sl[cs[i]], :], dfk[i]))) for i in every]
        lo, hi = sl[cs[-1]].start, sl[cs[0]].stop
        gq = gq + dot(q_ref[lo:hi, :], rows(*yq[::-1]), TN)
        gk = gk + dot(kv_ref[lo:hi, :HD], rows(*yk[::-1]), TN)

    def fold(g):
        g = g[:, :128] + g[:, 128:]
        return g.T[:FEAT] - g.T[FEAT:]

    gq_ref[...] = fold(gq)
    gk_ref[...] = fold(gk)


def query_features_kernel(mine_ref, q_ref, w_ref, f_ref):
    w = signed_pair(w_ref[0])
    sl = [slice(at, at + CHUNK) for at in range(0, q_ref.shape[0], CHUNK)]
    for g in range(0, len(sl), TOGETHER):
        group = sl[g : g + TOGETHER]
        logits = [dot(lanes(*[q_ref[x, :]] * 2), w, NT) for x in group]
        fq = [phi(x) for x in logits]
        for x, f in zip(group, fq):
            f_ref[x, :] = f


IN_VMEM = pl.BlockSpec(memory_space=pltpu.VMEM)


def in_vmem(x):
    return pltpu.with_memory_space_constraint(x, pltpu.VMEM)


def query_features(mine, q, w):
    return pl.pallas_call(
        query_features_kernel,
        grid_spec=pltpu.PrefetchScalarGridSpec(
            num_scalar_prefetch=1,
            grid=(1,),
            in_specs=[IN_VMEM, head_block(w)],
            out_specs=IN_VMEM,
        ),
        out_shape=jax.ShapeDtypeStruct((q.shape[0], 2 * FEAT), f32),
        compiler_params=pltpu.CompilerParams(vmem_limit_bytes=48 << 20),
        name="query_features",
    )(mine, in_vmem(q), w)


def key_features(kv_ref, wk, fk_s, st_s):
    one = jnp.ones((CHUNK, 128), bf16)
    state = jnp.zeros((2 * FEAT, 256), f32)
    count = kv_ref.shape[0] // CHUNK
    sl = [slice(c * CHUNK, (c + 1) * CHUNK) for c in range(count)]
    for g in range(0, count, TOGETHER):
        cs = range(g, min(g + TOGETHER, count))
        lk = [dot(lanes(*[kv_ref[sl[c], :HD]] * 2), wk, NT) for c in cs]
        fk = [phi(x) for x in lk]
        add = [dot(f.astype(bf16), lanes(kv_ref[sl[c], HD:], one), TN) for f, c in zip(fk, cs)]
        for i, c in enumerate(cs):
            fk_s[sl[c], :] = fk[i]
            st_s[c] = state.astype(bf16)
            state = state + add[i]


def assemble(mine, pieces, kv_ref):
    tok = pieces[0].shape[0]
    y, z, core = mine // 4, mine // 2 % 2, mine % 2
    spans = len(pieces) // 4
    for n, piece in enumerate(pieces):
        side, d = divmod(n, spans)
        from_y = (y + spans - d) % spans
        from_z = z if side % 2 == 0 else 1 - z
        from_core = core if side < 2 else 1 - core
        at = pl.multiple_of((from_y * 4 + from_z * 2 + from_core) * tok, tok)
        kv_ref[pl.ds(at, tok), :] = piece[...]


def layer_kernel(mine_ref, q_ref, fq_s, *refs):
    *pieces, wk_ref, gq_ref, gk_ref, kv_s, o_s, score, fk_s, st_s = refs
    assemble(mine_ref[0], pieces, kv_s)
    key_features(kv_s, signed_pair(wk_ref[0]), fk_s, st_s)
    teach(q_ref, kv_s, o_s, score, CHUNK)
    learn(q_ref, kv_s, o_s, fq_s, fk_s, st_s, gq_ref, gk_ref)


def layer(mine, q, fq, pieces, wk):
    total = q.shape[0]
    out = [jax.ShapeDtypeStruct((FEAT, HD), f32)] * 2
    return pl.pallas_call(
        layer_kernel,
        grid_spec=pltpu.PrefetchScalarGridSpec(
            num_scalar_prefetch=1,
            grid=(1,),
            in_specs=[IN_VMEM] * (2 + len(pieces)) + [head_block(wk)],
            out_specs=[whole(o) for o in out],
            scratch_shapes=[
                pltpu.VMEM((total, 2 * HD), bf16),
                pltpu.VMEM((total, HD), bf16),
                pltpu.VMEM((2, CHUNK, total), f32),
                pltpu.VMEM((total, 2 * FEAT), f32),
                pltpu.VMEM((total // CHUNK, 2 * FEAT, 256), bf16),
            ],
        ),
        out_shape=out,
        compiler_params=pltpu.CompilerParams(vmem_limit_bytes=48 << 20),
        name="layer",
    )(mine, *(in_vmem(a) for a in (q, fq, *pieces)), wk)


def step(x, move):
    return lax.ppermute(x, "seq", [(i, move(i)) for i in range(lax.axis_size("seq"))])


def shards(queries, keys, values, query_map, key_map):
    tok = queries.shape[0]
    peers = lax.axis_size("seq")
    mine = lax.axis_index("seq")
    here = lanes(keys, values)
    pieces = [here] + [step(here, lambda i, d=d: (i + 4 * d) % peers) for d in range(1, peers // 4)]
    over = [step(x, lambda i: i ^ 2) for x in pieces]
    qs = queries.reshape(tok, peers, HD).transpose(1, 0, 2)
    q = lax.all_to_all(qs, "seq", 0, 0, tiled=True).reshape(peers * tok, HD)
    index = mine.astype(jnp.int32).reshape(1)
    fq = query_features(index, q, query_map.transpose(0, 2, 1))
    fq, over[-1] = lax.optimization_barrier((fq, over[-1]))
    pieces = pieces + over
    pieces = pieces + [step(x, lambda i: i ^ 1) for x in pieces]
    gq, gk = layer(index, q, fq, pieces, key_map.transpose(0, 2, 1))
    return gq.T[None], gk.T[None]


def solution(mesh):
    return jax.shard_map(
        shards,
        mesh=mesh,
        in_specs=(
            P("seq", "kv"),
            P("seq", "kv"),
            P("seq", "kv"),
            P("kv", None, None),
            P("kv", None, None),
        ),
        out_specs=(P(("kv", "seq"), None, None), P(("kv", "seq"), None, None)),
        check_vma=False,
    )
```
